32 devices in a mesh: dp: 2 (over y), ulysses: 4 (over z), ep: 4 (over x, core).
Axes of the slice: x: 2, y: 2, z: 4, core: 2. Of those that a mesh axis runs over, the one named last changes fastest.
Arguments:
- tokens: bfloat16 [8, 1536, 768], P(('dp', 'ep'), 'ulysses'), may hold values from -6 to 6
- lengths: int32 [8, 2], P(('dp', 'ep')), may hold values from 1 to 1152, 1536 in all within a row
- permutation: int32 [16], replicated, may hold values from 0 to 15, each once
- routes: int32 [8, 1536, 2], P(('dp', 'ep'), 'ulysses'), may hold values from 0 to 3, all different within a row; in each aligned block of 384 rows (0 to 383, 384 to 767, ..., all dimensions but the last counted through in order) at most 288 rows name the same one
- cotangent: bfloat16 [8, 1536, 768], P(('dp', 'ep'), 'ulysses'), may hold values from -6 to 6
- attention_gain: bfloat16 [768], P('ep'), may hold values from 0.5 to 1.5
- attention_in: bfloat16 [768, 2304], P('ep'), may hold values from -0.3125 to 0.3125
- attention_out: bfloat16 [768, 768], P('ep'), may hold values from -1.25 to 1.25
- feed_gain: bfloat16 [768], P('ep'), may hold values from 0.5 to 1.5
- router_weight: bfloat16 [768, 4], P('ep'), may hold values from -0.15625 to 0.15625
- shared_in: bfloat16 [768, 4096], P('ep'), may hold values from -0.21875 to 0.21875
- shared_out: bfloat16 [2048, 768], P('ep'), may hold values from -0.1875 to 0.1875
- expert_in: bfloat16 [4, 768, 4096], P('ep'), may hold values from -0.21875 to 0.21875
- expert_out: bfloat16 [4, 2048, 768], P('ep'), may hold values from -0.25 to 0.25
Outputs:
- output: bfloat16 [8, 1536, 768], P(('dp', 'ep'), 'ulysses')
- grad_tokens: float32 [8, 1536, 768], P(('dp', 'ep'), 'ulysses')
- grad_attention_gain: float32 [768], P('ep')
- grad_attention_in: float32 [768, 2304], P('ep')
- grad_attention_out: float32 [768, 768], P('ep')
- grad_feed_gain: float32 [768], P('ep')
- grad_router: float32 [768, 4], P('ep')
- grad_shared_in: float32 [768, 4096], P('ep')
- grad_shared_out: float32 [2048, 768], P('ep')
- grad_expert_in: float32 [4, 768, 4096], P('ep', None, 'ulysses')
- grad_expert_out: float32 [4, 2048, 768], P('ep', 'ulysses')
The draws below stay inside these ranges and needn't reach their ends.
Inputs may be any that keep to these rules, and one draw needn't show every extreme that they name: Each row holds the lengths of the 2 sequences of one pack; they sum to 1536 and the largest is at most 1152. a permutation of the 16 sequences, numbered pack by pack. `routes`: each row names 2 different experts.
All inputs are finite; a program needn't handle non-finite values.
Results may differ from the reference program's by a relative error of at most 0.014.
The reference program's roundings to bfloat16 on the way count: a program that leaves them out, or rounds other values in their place, can miss the bound.
Values may be sent and summed in bfloat16 or wider, within the bound.
No kernel may reach another device: no remote copies, remote signals or barrier semaphores. Data moves between devices by JAX's collectives and lax.ppermute only.
A program may use at most 192 MiB of HBM per device.

```python
import math
import jax
import jax.numpy as jnp
import numpy as np
from jax import lax

D = 768
HEADS = 12
HEAD_DIM = 64
EFF = 2048
SHARED = 2048
TOP = 2
SEQS = 2
TOK_DEV = 384
PACK = 1536
PACKS = 8
EXPERTS = 4
NSEQ = 16
MAXLEN = 1152
CAP = 216
N_ULYSSES = 4


def steps_of(rng, shape, cuts, smallest, top_value):
    def one(dim, parts):
        steps = jax.random.uniform(jax.random.fold_in(jax.random.fold_in(rng, 6), dim), (parts,), jnp.float32, smallest / len(cuts), top_value / len(cuts))
        return jnp.repeat(jnp.exp(steps), shape[dim] // parts).reshape((-1,) + (1,) * (len(shape) - dim - 1))

    factor_of = one(*cuts[0])
    for cut in cuts[1:]:
        factor_of = factor_of * one(*cut)
    return factor_of


def length_profile(amount, total, most, slope):
    weights = [(1 << 20) // math.isqrt(standing ** slope) + 1 for standing in range(2, amount + 1)]
    surplus, counts = total - most - (amount - 1), [1] * (amount - 1)
    while surplus > 0:
        movable = [i for i in range(amount - 1) if counts[i] < most]
        whole, left = sum([weights[i] for i in movable]), surplus
        for i in movable:
            more = min(most - counts[i], max(1, left * weights[i] // whole), surplus)
            counts[i] = counts[i] + more
            surplus = surplus - more
    return np.array([most] + counts)


def ragged(key, amount, total, most, skew):
    if amount == 2:
        one = jax.random.randint(key, (), max(1, total - most), min(most, total - 1) + 1)
        return jnp.stack([one, total - one])
    sizes = jnp.asarray(length_profile(amount, total, most, skew), jnp.int32)
    pairs = (amount - 1) // 2
    giver, receiver = sizes[1:1 + 2 * pairs:2], sizes[2:2 + 2 * pairs:2]
    slack = jnp.minimum(giver - 1, most - receiver)
    passed = jax.random.randint(jax.random.fold_in(key, 1), (pairs,), 0, 1 << 20) % (slack + 1)
    sizes = sizes.at[1:1 + 2 * pairs:2].set(giver - passed).at[2:2 + 2 * pairs:2].set(receiver + passed)
    return sizes[jax.random.permutation(jax.random.fold_in(key, 2), amount)]


def assign_block(rng, own, number, rows, number_of, top, bound, lean):
    ranking = jax.random.permutation(rng, number_of)
    heavy_load, common = portions_of(number_of, rows * top, bound, lean, True), portions_of(number_of, rows * top, bound, lean, False)
    places = jnp.arange(number_of)

    def named(sizes, offset_by):
        used = int((sizes > 0).sum())
        fixed = max(1, used // 4)
        moved = fixed + (places - fixed + offset_by * (used - fixed)) % max(1, number_of - fixed)
        return jnp.zeros((number_of,), jnp.int32).at[ranking[jnp.where(places < fixed, places, moved)]].set(jnp.asarray(sizes, jnp.int32))

    sizes = jnp.where(number % 4 == 0, named(heavy_load, number // 4), named(common, number - number // 4 - 1))
    mixed = jax.random.permutation(jax.random.fold_in(own, 3), number_of)
    giver, sink = mixed[0:number_of // 2 * 2:2], mixed[1:number_of // 2 * 2:2]
    room = jnp.minimum(sizes[giver] - 1, bound - sizes[sink]) // 2
    room = jnp.where((giver == ranking[0]) | (sink == ranking[0]) | (sizes[sink] == 0), 0, jnp.maximum(room, 0))
    moved = jax.random.randint(jax.random.fold_in(own, 4), (number_of // 2,), 0, 1 << 20) % (room + 1)
    sizes = sizes.at[giver].add(-moved).at[sink].add(moved)
    members = jnp.searchsorted(jnp.cumsum(sizes), jnp.arange(rows * top), side="right").astype(jnp.int32)
    table = members.reshape(top, rows).T
    table = table[jax.random.permutation(jax.random.fold_in(own, 1), rows)]
    offset_by = jax.random.randint(jax.random.fold_in(own, 2), (rows, 1), 0, top)
    return jnp.take_along_axis(table, (jnp.arange(top)[None, :] + offset_by) % top, axis=1)


def portions_of(number_of, total, bound, skew, full):
    weights = [(1 << 20) // math.isqrt(rank ** skew) + 1 for rank in range(1, number_of + 1)]
    largest = bound if full else min(bound, max(-(-total // number_of), total * weights[0] // sum(weights)))
    least = 1 if total - largest >= number_of - 1 else 0
    holding, spare = [largest] + [least] * (number_of - 1), total - largest - least * (number_of - 1)
    while spare > 0:
        free = [i for i in range(1, number_of) if holding[i] < largest] or [i for i in range(1, number_of) if holding[i] < bound]
        whole, left = sum([weights[i] for i in free]), spare
        for i in free:
            more = min(bound - holding[i], max(1, left * weights[i] // whole), spare)
            holding[i] = holding[i] + more
            spare = spare - more
    return np.array(holding)


def noise(key, shape, spread, reach, pieces=(), kind=jnp.bfloat16):
    level = steps_of(key, shape, pieces, -0.22, 0.18) if pieces else 1.0
    drawn = jax.random.normal(key, shape, jnp.float32) * spread * level
    return jnp.minimum(jnp.maximum(drawn, -reach), reach).astype(kind)


def setup_inputs(seed: int = 0) -> dict:
    key_list = jax.random.split(jax.random.key(seed), 15)
    tokens = noise(key_list[0], (PACKS, PACK, D), 1.0, 6.0, ((0, 8), (1, 4)))
    lengths = jax.vmap(lambda own: ragged(own, SEQS, PACK, MAXLEN, 2))(jax.random.split(key_list[1], PACKS)).reshape((PACKS, SEQS)).astype(jnp.int32)
    permutation = jax.random.permutation(key_list[2], NSEQ).astype(jnp.int32)
    routes_keys = jax.random.split(jax.random.fold_in(key_list[3], 1), PACKS * PACK // TOK_DEV)
    routes_turns = jax.random.permutation(jax.random.fold_in(key_list[3], 3), PACKS * PACK // TOK_DEV)
    routes = jax.vmap(lambda own, number: assign_block(jax.random.fold_in(key_list[3], 2), own, number, TOK_DEV, EXPERTS, TOP, CAP + CAP // 3, 1))(routes_keys, routes_turns).reshape((PACKS, PACK, TOP))
    cotangent = noise(key_list[4], (PACKS, PACK, D), 1.0, 6.0, ((0, 8), (1, 4)))
    attention_gain = jnp.clip(1.0 + 0.1 * jax.random.normal(key_list[5], (D,), jnp.float32), 0.5, 1.5).astype(jnp.bfloat16)
    attention_in = noise(key_list[6], (D, 3 * D), (D // 2) ** -0.5, 0.3125, ((0, 4),))
    attention_out = noise(key_list[7], (D, D), (D // 32) ** -0.5, 1.25, ((0, 4),))
    feed_gain = jnp.clip(1.0 + 0.1 * jax.random.normal(key_list[8], (D,), jnp.float32), 0.5, 1.5).astype(jnp.bfloat16)
    router_weight = noise(key_list[9], (D, EXPERTS), (2 * D) ** -0.5, 0.15625, ((0, 4),))
    shared_in = noise(key_list[10], (D, 2 * SHARED), D ** -0.5, 0.21875, ((0, 4),))
    shared_out = noise(key_list[11], (SHARED, D), (SHARED // 2) ** -0.5, 0.1875, ((0, 4),))
    expert_in = noise(key_list[12], (EXPERTS, D, 2 * EFF), D ** -0.5, 0.21875, ((0, 4),))
    expert_out = noise(key_list[13], (EXPERTS, EFF, D), (EFF // 4) ** -0.5, 0.25, ((0, 4),))
    return dict(tokens=tokens, lengths=lengths, permutation=permutation, routes=routes, cotangent=cotangent, attention_gain=attention_gain, attention_in=attention_in, attention_out=attention_out, feed_gain=feed_gain, router_weight=router_weight, shared_in=shared_in, shared_out=shared_out, expert_in=expert_in, expert_out=expert_out)


@jax.custom_vjp
def low(v):
    return lax.optimization_barrier(v.astype(jnp.bfloat16)).astype(jnp.float32)

@jax.custom_vjp
def low_back(v):
    return v

def low_keep(v):
    return (low(v), None)

def low_pass(kept, grad):
    return (grad,)

def back_keep(v):
    return (v, None)

def back_low(kept, grad):
    return (low(grad),)
low.defvjp(low_keep, low_pass)
low_back.defvjp(back_keep, back_low)
epsilon = 1e-06
base_freq = 10000.0
neg_fill = -1e+30
highest = lax.Precision.HIGHEST

def product(left, right):
    return jnp.dot(left, right, precision=highest)

def rms_norm(value, gain):
    scale = lax.rsqrt(lax.optimization_barrier(jnp.mean(value * value, axis=-1, keepdims=True)) + epsilon)
    return value * scale * gain

def rotary(value, position):
    half = value.shape[-1] // 2
    freq = base_freq ** (-(jnp.arange(half, dtype=jnp.float32) * 2.0) / value.shape[-1])
    angle = position.astype(jnp.float32)[:, None] * freq[None, :]
    cosine = jnp.cos(angle)[:, None, :]
    sine = jnp.sin(angle)[:, None, :]
    first = value[..., :half]
    second = value[..., half:]
    return jnp.concatenate([first * cosine - second * sine, second * cosine + first * sine], axis=-1)

def swiglu(pair):
    half = pair.shape[-1] // 2
    return jax.nn.silu(pair[..., :half]) * pair[..., half:]

def seq_layout(length_row, count):
    ends = jnp.cumsum(length_row).astype(jnp.int32)
    starts = ends - length_row
    index = jnp.arange(count, dtype=jnp.int32)
    segment = lax.optimization_barrier(jnp.sum((index[:, None] >= ends[None, :]).astype(jnp.int32), axis=1, dtype=jnp.int32))
    which = segment[:, None] == jnp.arange(length_row.shape[0], dtype=jnp.int32)[None, :]
    position = index - lax.optimization_barrier(jnp.sum(jnp.where(which, starts[None, :], 0), axis=1, dtype=jnp.int32))
    return (segment, position, which)

def capacity_plan(priority, route_rows):
    member = lax.optimization_barrier(jnp.sum((route_rows[:, :, None] == jnp.arange(EXPERTS, dtype=jnp.int32)[None, None, :]).astype(jnp.float32), axis=1))
    earlier = (priority[None, :] < priority[:, None]).astype(jnp.float32)
    rank = product(earlier, member)
    keep = member * (rank < CAP).astype(jnp.float32)
    slots = jnp.arange(CAP, dtype=jnp.float32)
    return keep.T[:, None, :] * (rank.T[:, None, :] == slots[None, :, None]).astype(jnp.float32)

def attend(query, keys, values, segment):
    rows = query.shape[0]
    block = min(512, rows)
    count = rows // block
    index = jnp.arange(rows, dtype=jnp.int32)
    scale = HEAD_DIM ** (-0.5)

    def one_block(item):
        query_block, segment_block, index_block = item
        scores = low_back(jnp.einsum('qhd,khd->hqk', query_block, keys, precision=highest) * scale)
        allowed = (segment_block[:, None] == segment[None, :]) & (index_block[:, None] >= index[None, :])
        scores = jnp.where(allowed[None], scores, neg_fill)
        peak = lax.optimization_barrier(jnp.max(scores, axis=-1, keepdims=True))
        weight = jnp.exp(scores - peak)
        prob = weight / lax.optimization_barrier(jnp.sum(weight, axis=-1, keepdims=True))
        return jnp.einsum('hqk,khd->qhd', low(prob), values, precision=highest)
    result = lax.map(jax.checkpoint(one_block), (query.reshape(count, block, HEADS, HEAD_DIM), segment.reshape(count, block), index.reshape(count, block)))
    return result.reshape(rows, HEADS, HEAD_DIM)

def pack_forward(x_pack, length_row, route_rows, pack_id, permutation, gain_first, mix_in, mix_out, gain_second, router, shared_up, shared_down, experts_up, experts_down):
    segment, position, which = seq_layout(length_row, PACK)
    normed = low(rms_norm(x_pack, gain_first))
    mixed = low_back(low(product(normed, mix_in)))
    query = low(rotary(mixed[:, :D].reshape(PACK, HEADS, HEAD_DIM), position))
    keys = low(rotary(mixed[:, D:2 * D].reshape(PACK, HEADS, HEAD_DIM), position))
    values = mixed[:, 2 * D:].reshape(PACK, HEADS, HEAD_DIM)
    attended = low_back(low(attend(query, keys, values, segment).reshape(PACK, D)))
    residual = x_pack + low_back(product(attended, mix_out))
    feed = low(rms_norm(residual, gain_second))
    probs = jax.nn.softmax(product(feed, router), axis=-1)
    seq_rank = lax.dynamic_slice_in_dim(permutation, pack_id * SEQS, SEQS)
    order = lax.optimization_barrier(jnp.sum(jnp.where(which, seq_rank[None, :], 0), axis=1, dtype=jnp.int32)) * PACK + jnp.arange(PACK, dtype=jnp.int32)
    select = jax.vmap(capacity_plan)(order.reshape(N_ULYSSES, TOK_DEV), route_rows.reshape(N_ULYSSES, TOK_DEV, TOP))
    feed_blocks = feed.reshape(N_ULYSSES, TOK_DEV, D)
    slots = low_back(jnp.einsum('beci,bid->becd', select, feed_blocks, precision=highest))
    pair = low_back(jnp.einsum('becd,edf->becf', slots, experts_up, precision=highest))
    hidden = low(swiglu(pair))
    result = low_back(low(jnp.einsum('becf,efd->becd', hidden, experts_down, precision=highest)))
    per_expert = jnp.einsum('beci,becd->beid', select, result, precision=highest)
    mixture = jnp.einsum('bie,beid->bid', probs.reshape(N_ULYSSES, TOK_DEV, EXPERTS), per_expert, precision=highest).reshape(PACK, D)
    shared_pair = low_back(product(feed, shared_up))
    shared_hidden = low(swiglu(shared_pair))
    shared_result = low_back(product(shared_hidden, shared_down))
    return residual + mixture + shared_result

def reference(tokens, lengths, permutation, routes, cotangent, attention_gain, attention_in, attention_out, feed_gain, router_weight, shared_in, shared_out, expert_in, expert_out):
    floats = tuple((array.astype(jnp.float32) for array in (tokens, attention_gain, attention_in, attention_out, feed_gain, router_weight, shared_in, shared_out, expert_in, expert_out)))
    pack_ids = jnp.arange(PACKS, dtype=jnp.int32)
    layer = jax.checkpoint(pack_forward)

    def forward(inputs, *params):

        def step(carry, item):
            x_pack, length_row, route_rows, pack_id = item
            return (carry, layer(x_pack, length_row, route_rows, pack_id, permutation, *params))
        _, result = lax.scan(step, jnp.zeros((), jnp.float32), (inputs, lengths, routes, pack_ids))
        return result
    result, pull = jax.vjp(forward, *floats)
    grads = pull(cotangent.astype(jnp.float32))
    return (result.astype(jnp.bfloat16), grads[0], grads[1], grads[2], grads[3], grads[4], grads[5], grads[6], grads[7], grads[8], grads[9])
```

```python
import functools

import jax
import jax.numpy as jnp
from jax import lax
from jax.experimental import pallas as pl
from jax.experimental.pallas import tpu as pltpu
from jax.sharding import PartitionSpec as P

HEAD_DIM = 64
epsilon = 1e-06
base_freq = 10000.0
neg_fill = -1e30
highest = lax.Precision.HIGHEST
bf16 = jnp.bfloat16
f32 = jnp.float32
QB = 512
KB = 512


def dot(a, b, ca=1, cb=0, precision=None):
    return lax.dot_general(
        a, b, (((ca,), (cb,)), ((), ())), preferred_element_type=f32, precision=precision
    )


def swap(x, axis, k):
    n = lax.axis_size(axis)
    return lax.ppermute(x, axis, [(i, i ^ k) for i in range(n)])


def whole(shape):
    zeros = (0,) * len(shape)
    return pl.BlockSpec(shape, lambda *_: zeros)


def kernel_call(body, grid, scalars, ins, in_specs, outs, out_specs, scratch=(), flops=0, name=None):
    moved = sum(x.size * x.dtype.itemsize for x in list(ins) + list(outs))
    return pl.pallas_call(
        body,
        out_shape=tuple(outs),
        grid_spec=pltpu.PrefetchScalarGridSpec(
            num_scalar_prefetch=len(scalars),
            grid=grid,
            in_specs=list(in_specs),
            out_specs=tuple(out_specs),
            scratch_shapes=list(scratch),
        ),
        cost_estimate=pl.CostEstimate(flops=int(flops), transcendentals=0, bytes_accessed=int(moved)),
        compiler_params=pltpu.CompilerParams(
            dimension_semantics=("arbitrary",) * len(grid), vmem_limit_bytes=60 << 20
        ),
        name=name,
    )(*scalars, *ins)


def sds(shape, dtype=f32):
    return jax.ShapeDtypeStruct(shape, dtype)


def swap_halves(m):
    width = m.shape[1]
    lane = lax.broadcasted_iota(jnp.int32, m.shape, 1) % HEAD_DIM
    back = pltpu.roll(m, width - HEAD_DIM // 2, 1)
    ahead = pltpu.roll(m, HEAD_DIM // 2, 1)
    return jnp.where(lane < HEAD_DIM // 2, back, ahead)


def silu_parts(gate):
    sig = 1.0 / (1.0 + jnp.exp(-gate))
    return gate * sig, sig * (1.0 + gate * (1.0 - sig))


def qkv_body(sc, x0, x1, x2, x3, w0, w1, w2, w3, gain, cos, sin, q, k, kt, v, vt, at, wscr, xscr):
    step = pl.program_id(0)
    heads = q.shape[0]
    wide = heads * HEAD_DIM
    part = w0.shape[0]

    @pl.when(step == 0)
    def _():
        for j, w in enumerate((w0, w1, w2, w3)):
            wscr[pl.ds(pl.multiple_of(sc[4 + j] * part, 16), part), :] = w[...]

    for j, x in enumerate((x0, x1, x2, x3)):

        @pl.when(step == j)
        def _(x=x):
            xscr[...] = x[...].astype(f32)

    x = xscr[...]
    scale = lax.rsqrt(jnp.mean(x * x, axis=-1, keepdims=True) + epsilon)
    a = (x * scale * gain[...]).astype(bf16)
    at[...] = a.T
    mixed = dot(a, wscr[...]).astype(bf16)
    qk = mixed[:, : 2 * wide].astype(f32)
    copies = 2 * wide // cos.shape[1]
    c = jnp.concatenate([cos[...]] * copies, axis=1)
    s = jnp.concatenate([sin[...]] * copies, axis=1)
    turned = (qk * c + swap_halves(qk) * s).astype(bf16)
    for h in range(heads):
        q[h] = turned[:, h * HEAD_DIM : (h + 1) * HEAD_DIM] * jnp.asarray(HEAD_DIM**-0.5, bf16)
        kh = turned[:, wide + h * HEAD_DIM : wide + (h + 1) * HEAD_DIM]
        k[h] = kh
        kt[h] = kh.T
        vh = mixed[:, 2 * wide + h * HEAD_DIM : 2 * wide + (h + 1) * HEAD_DIM]
        v[h] = vh
        vt[h] = vh.T


def qkv(sc, xs, ws, gain, cos, sin, heads):
    rows, width = xs[0].shape
    total = rows * len(xs)
    wide = heads * HEAD_DIM
    row3 = pl.BlockSpec((heads, rows, HEAD_DIM), lambda i, s: (0, s[i], 0))
    lane3 = pl.BlockSpec((heads, HEAD_DIM, rows), lambda i, s: (0, 0, s[i]))
    table = pl.BlockSpec((rows, cos.shape[1]), lambda i, s: (s[i], 0))
    return kernel_call(
        qkv_body,
        (len(xs),),
        (sc,),
        (*xs, *ws, gain, cos, sin),
        [whole(x.shape) for x in xs] + [whole(w.shape) for w in ws] + [whole(gain.shape), table, table],
        (
            sds((heads, total, HEAD_DIM), bf16),
            sds((heads, total, HEAD_DIM), bf16),
            sds((heads, HEAD_DIM, total), bf16),
            sds((heads, total, HEAD_DIM), bf16),
            sds((heads, HEAD_DIM, total), bf16),
            sds((width, total), bf16),
        ),
        (row3, row3, lane3, row3, lane3, pl.BlockSpec((width, rows), lambda i, s: (0, s[i]))),
        scratch=[pltpu.VMEM((width, 3 * wide), bf16), pltpu.VMEM((rows, width), f32)],
        flops=2 * total * width * 3 * wide,
        name="qkv",
    )


def masked(scores, key_start, query_start, starts):
    keys = lax.broadcasted_iota(jnp.int32, scores.shape, 0) + key_start
    queries = lax.broadcasted_iota(jnp.int32, scores.shape, 1) + query_start
    return jnp.where((keys >= starts) & (keys <= queries), scores, neg_fill)


def attend_body(sc, lo, q, k, vt, starts, out0, out1, out2, out3, o, lse, oscr):
    heads, rows, _ = q.shape
    count = rows // QB
    for h in range(heads):

        def block(i, _, h=h):
            q_at = pl.multiple_of(i * QB, QB)
            query = q[h, pl.ds(q_at, QB), :]
            start_row = starts[0:1, pl.ds(q_at, QB)]

            def step(j, carry):
                top, total, acc = carry
                k_at = pl.multiple_of(j * KB, KB)
                scores = dot(k[h, pl.ds(k_at, KB), :], query, 1, 1)
                scores = masked(scores, k_at, q_at, start_row)
                new = jnp.maximum(top, jnp.max(scores, axis=0, keepdims=True))
                weight = jnp.exp(scores - new)
                fade = jnp.exp(top - new)
                total = total * fade + jnp.sum(weight, axis=0, keepdims=True)
                acc = acc * fade + dot(vt[h, :, pl.ds(k_at, KB)], weight.astype(bf16))
                return new, total, acc

            top, total, acc = lax.fori_loop(
                lo[i],
                (q_at + QB + KB - 1) // KB,
                step,
                (
                    jnp.full((1, QB), neg_fill, f32),
                    jnp.zeros((1, QB), f32),
                    jnp.zeros((HEAD_DIM, QB), f32),
                ),
            )
            result = (acc / total).T
            o[h, pl.ds(q_at, QB), :] = result
            oscr[pl.ds(q_at, QB), h * HEAD_DIM : (h + 1) * HEAD_DIM] = result
            lse[h, 0:1, pl.ds(q_at, QB)] = top + jnp.log(total)
            return 0

        lax.fori_loop(0, count, block, 0)
    part = out0.shape[0]
    for j, out in enumerate((out0, out1, out2, out3)):
        out[...] = oscr[pl.ds(pl.multiple_of(sc[j] * part, 16), part), :].astype(bf16)


def attend(sc, lo, q, k, vt, starts, part):
    heads, rows, _ = q.shape
    wide = heads * HEAD_DIM
    outs = [sds((part, wide), bf16)] * 4 + [sds((heads, rows, HEAD_DIM)), sds((heads, 8, rows))]
    return kernel_call(
        attend_body,
        (1,),
        (sc, lo),
        (q, k, vt, starts),
        [whole(x.shape) for x in (q, k, vt, starts)],
        outs,
        [whole(x.shape) for x in outs],
        scratch=[pltpu.VMEM((rows, wide), f32)],
        flops=heads * rows * rows * 4 * HEAD_DIM * 4,
        name="attend",
    )


def attend_back_body(
    sc, hi, q, k, kt, v, lse, o, starts, g0, g1, g2, g3, cos, sin,
    out0, out1, out2, out3, mixed, do, delta, dqt, dk, dv, mscr,
):
    heads, rows, _ = q.shape
    wide = heads * HEAD_DIM
    part = g0.shape[0]
    count = rows // KB
    ones = jnp.ones((8, HEAD_DIM), f32)
    for j, g in enumerate((g0, g1, g2, g3)):
        for h in range(heads):
            do[h, pl.ds(pl.multiple_of(sc[j] * part, 16), part), :] = g[
                :, h * HEAD_DIM : (h + 1) * HEAD_DIM
            ].astype(f32)
    for h in range(heads):
        delta[...] = dot(ones, do[h] * o[h], 1, 1, highest)
        dqt[...] = jnp.zeros(dqt.shape, f32)

        def block(j, _, h=h):
            k_at = pl.multiple_of(j * KB, KB)
            key = k[h, pl.ds(k_at, KB), :]
            key_t = kt[h, :, pl.ds(k_at, KB)]
            value = v[h, pl.ds(k_at, KB), :]
            dk[...] = jnp.zeros(dk.shape, f32)
            dv[...] = jnp.zeros(dv.shape, f32)

            def step(i, _):
                q_at = pl.multiple_of(i * QB, QB)
                query = q[h, pl.ds(q_at, QB), :]
                grad = do[h, pl.ds(q_at, QB), :].astype(bf16)
                scores = dot(key, query, 1, 1)
                scores = masked(scores, k_at, q_at, starts[0:1, pl.ds(q_at, QB)])
                prob = jnp.exp(scores - lse[h, 0:1, pl.ds(q_at, QB)])
                grad_prob = dot(value, grad, 1, 1)
                grad_score = (prob * (grad_prob - delta[0:1, pl.ds(q_at, QB)])).astype(bf16)
                dv[...] += dot(prob.astype(bf16), grad)
                dk[...] += dot(grad_score, query)
                dqt[:, pl.ds(q_at, QB)] += dot(key_t, grad_score)
                return 0

            lax.fori_loop(k_at // QB, hi[j], step, 0)
            mscr[pl.ds(k_at, KB), wide + h * HEAD_DIM : wide + (h + 1) * HEAD_DIM] = dk[...]
            mscr[pl.ds(k_at, KB), 2 * wide + h * HEAD_DIM : 2 * wide + (h + 1) * HEAD_DIM] = dv[...]
            return 0

        lax.fori_loop(0, count, block, 0)
        mscr[:, h * HEAD_DIM : (h + 1) * HEAD_DIM] = dqt[...].T * (HEAD_DIM**-0.5)
    copies = 2 * wide // cos.shape[1]

    def finish(r, _):
        at = pl.multiple_of(r * part, 128)
        here = pl.ds(at, part)
        qk = mscr[here, : 2 * wide]
        c = jnp.concatenate([cos[here, :]] * copies, axis=1)
        s = jnp.concatenate([sin[here, :]] * copies, axis=1)
        mixed[here, : 2 * wide] = (qk * c - swap_halves(qk) * s).astype(bf16)
        mixed[here, 2 * wide :] = mscr[here, 2 * wide :].astype(bf16)
        return 0

    lax.fori_loop(0, rows // part, finish, 0)
    for j, out in enumerate((out0, out1, out2, out3)):
        out[...] = mixed[pl.ds(pl.multiple_of(sc[j] * part, 16), part), :]


def attend_back(sc, hi, q, k, kt, v, lse, o, starts, grads, cos, sin):
    heads, rows, _ = q.shape
    wide = heads * HEAD_DIM
    part = grads[0].shape[0]
    ins = (q, k, kt, v, lse, o, starts, *grads, cos, sin)
    outs = [sds((part, 3 * wide), bf16)] * 4 + [sds((rows, 3 * wide), bf16)]
    return kernel_call(
        attend_back_body,
        (1,),
        (sc, hi),
        ins,
        [whole(x.shape) for x in ins],
        outs,
        [whole(x.shape) for x in outs],
        scratch=[
            pltpu.VMEM((heads, rows, HEAD_DIM), f32),
            pltpu.VMEM((8, rows), f32),
            pltpu.VMEM((HEAD_DIM, rows), f32),
            pltpu.VMEM((KB, HEAD_DIM), f32),
            pltpu.VMEM((KB, HEAD_DIM), f32),
            pltpu.VMEM((rows, 3 * wide), f32),
        ],
        flops=heads * rows * rows * 10 * HEAD_DIM * 4,
        name="attend_back",
    )


def mixed_weight_grad_body(sc, at, mixed, keep, send):
    part = keep.shape[1]
    for j, (out, slot) in enumerate(((keep, 0), (send, 0), (keep, 1), (send, 1))):
        left = at[pl.ds(pl.multiple_of(sc[4 + j] * part, 16), part), :]
        out[slot] = dot(left, mixed[...]).astype(bf16)


def mixed_weight_grad(sc, at, mixed):
    part = at.shape[0] // 4
    outs = [sds((2, part, mixed.shape[1]), bf16)] * 2
    return kernel_call(
        mixed_weight_grad_body,
        (1,),
        (sc,),
        (at, mixed),
        [whole(at.shape), whole(mixed.shape)],
        outs,
        [whole(x.shape) for x in outs],
        flops=2 * at.size * mixed.shape[1],
        name="mixed_weight_grad",
    )


def feed_body(
    sc, c0, c1, c2, c3, w0, w1, w2, w3, x, gain, router, sel, cot,
    residual, b, bt, probs, s0, s1, s2, s3, z0, z1, z2, z3, wscr,
):
    part = w0.shape[0]
    for j, w in enumerate((w0, w1, w2, w3)):
        wscr[pl.ds(pl.multiple_of(sc[4 + j] * part, 16), part), :] = w[...]
    acc = x[...].astype(f32)
    head = c0.shape[1]
    for j, ctx in enumerate((c0, c1, c2, c3)):
        acc = acc + dot(ctx[...], wscr[pl.ds(pl.multiple_of(sc[j] * head, 16), head), :])
    residual[...] = acc
    scale = lax.rsqrt(jnp.mean(acc * acc, axis=-1, keepdims=True) + epsilon)
    feed = (acc * scale * gain[...]).astype(bf16)
    b[...] = feed
    bt[...] = feed.T
    logits = dot(feed, router[...])
    live = lax.broadcasted_iota(jnp.int32, logits.shape, 1) < 4
    logits = jnp.where(live, logits, neg_fill)
    weight = jnp.exp(logits - jnp.max(logits, axis=-1, keepdims=True))
    p = weight / jnp.sum(weight, axis=-1, keepdims=True)
    probs[...] = p
    p1 = p.astype(bf16)
    rest = p - p1.astype(f32)
    p2 = rest.astype(bf16)
    p3 = (rest - p2.astype(f32)).astype(bf16)
    for j, (s, z) in enumerate(((s0, z0), (s1, z1), (s2, z2), (s3, z3))):
        pick = sel[j]
        s[...] = dot(pick, feed).astype(bf16)
        slot = dot(pick, p1) + dot(pick, p2) + dot(pick, p3)
        z[...] = (dot(pick, cot[...]) * slot[:, j : j + 1]).astype(bf16)


def feed(sc, ctx, ws, x, gain, router, sel, cot):
    rows, width = x.shape
    slots = sel.shape[1]
    ins = (*ctx, *ws, x, gain, router, sel, cot)
    outs = [
        sds((rows, width)),
        sds((rows, width), bf16),
        sds((width, rows), bf16),
        sds((rows, 128)),
    ] + [sds((slots, width), bf16)] * 8
    return kernel_call(
        feed_body,
        (1,),
        (sc,),
        ins,
        [whole(i.shape) for i in ins],
        outs,
        [whole(i.shape) for i in outs],
        scratch=[pltpu.VMEM((width, width), bf16)],
        flops=2 * rows * width * width + 16 * rows * slots * width,
        name="feed",
    )


def shared_body(
    sc, b, bt, c, g0, g1, g2, g3, u0, u1, u2, u3, o0, o1, o2, o3,
    res, back, in_keep, in_send, out_grad, wg, wu,
):
    step = pl.program_id(0)
    part = g0.shape[0]
    per = pl.num_programs(0) // 4
    for j, (g, u) in enumerate(((g0, u0), (g1, u1), (g2, u2), (g3, u3))):
        here = pl.ds(pl.multiple_of(sc[4 + j] * part, 16), part)
        wg[here, :] = g[...]
        wu[here, :] = u[...]

    @pl.when(step == 0)
    def _():
        res[...] = jnp.zeros(res.shape, f32)
        back[...] = jnp.zeros(back.shape, f32)

    x = b[...]
    cot = c[...]
    gate = dot(x, wg[...])
    up = dot(x, wu[...])
    act, dact = silu_parts(gate)
    hidden = (act * up).astype(bf16)
    down = jnp.where(
        step // per == 0,
        o0[...],
        jnp.where(step // per == 1, o1[...], jnp.where(step // per == 2, o2[...], o3[...])),
    )
    res[...] += dot(hidden, down)
    s = dot(cot, down, 1, 1)
    gate_grad = (s * up * dact).astype(bf16)
    up_grad = (s * act).astype(bf16)
    back[...] += dot(gate_grad, wg[...], 1, 1) + dot(up_grad, wu[...], 1, 1)
    out_grad[...] = dot(hidden.T, cot).astype(bf16)
    for j, (out, slot) in enumerate(((in_keep, 0), (in_send, 0), (in_keep, 1), (in_send, 1))):
        left = bt[pl.ds(pl.multiple_of(sc[4 + j] * part, 16), part), :]
        here = slice(slot * part, (slot + 1) * part)
        out[0, here, :] = dot(left, gate_grad).astype(bf16)
        out[1, here, :] = dot(left, up_grad).astype(bf16)


def shared(sc, b, bt, c, in_parts, out_parts):
    rows, width = b.shape
    part, double = in_parts[0].shape
    hidden = double // 2
    blk = 256
    per = hidden // 4 // blk
    steps = 4 * per
    at = lambda i, s: s[4 + i // per] * per + i % per
    gate = pl.BlockSpec((part, blk), lambda i, s: (0, at(i, s)))
    up = pl.BlockSpec((part, blk), lambda i, s: (0, steps + at(i, s)))
    downs = [
        pl.BlockSpec((blk, width), lambda i, s, k=k: (jnp.clip(i - k * per, 0, per - 1), 0))
        for k in range(4)
    ]
    grad_in = pl.BlockSpec((2, 2 * part, blk), lambda i, s: (0, 0, at(i, s)))
    outs = [
        sds((rows, width)),
        sds((rows, width)),
        sds((2, 2 * part, hidden), bf16),
        sds((2, 2 * part, hidden), bf16),
        sds((hidden, width), bf16),
    ]
    return kernel_call(
        shared_body,
        (steps,),
        (sc,),
        (b, bt, c, *in_parts, *in_parts, *out_parts),
        [whole(b.shape), whole(bt.shape), whole(c.shape)] + [gate] * 4 + [up] * 4 + downs,
        outs,
        [
            whole(outs[0].shape),
            whole(outs[1].shape),
            grad_in,
            grad_in,
            pl.BlockSpec((blk, width), lambda i, s: (i, 0)),
        ],
        scratch=[pltpu.VMEM((width, blk), bf16), pltpu.VMEM((width, blk), bf16)],
        flops=18 * rows * width * hidden,
        name="shared",
    )


def expert_body(x0, x1, x2, x3, wg, wu, wo, r0, r1, r2, r3, hidden, gates, ups, xt, xs, acc):
    step = pl.program_id(0)
    part = x0.shape[0]

    @pl.when(step == 0)
    def _():
        for j, x in enumerate((x0, x1, x2, x3)):
            xs[j * part : (j + 1) * part, :] = x[...]
        acc[...] = jnp.zeros(acc.shape, f32)
        xt[...] = xs[...].T

    x = xs[...]
    gate = dot(x, wg[...])
    up = dot(x, wu[...])
    gates[...] = gate
    ups[...] = up
    act, _ = silu_parts(gate)
    h = (act * up).astype(bf16)
    hidden[...] = h
    acc[...] += dot(h, wo[...])

    @pl.when(step == pl.num_programs(0) - 1)
    def _():
        for j, r in enumerate((r0, r1, r2, r3)):
            r[...] = acc[j * part : (j + 1) * part, :].astype(bf16)


def expert(xs, w_in, w_out):
    part, width = xs[0].shape
    rows = 4 * part
    hidden = w_out.shape[0]
    blk = 256
    steps = hidden // blk
    col = pl.BlockSpec((rows, blk), lambda i: (0, i))
    outs = [sds((part, width), bf16)] * 4 + [
        sds((rows, hidden), bf16),
        sds((rows, hidden)),
        sds((rows, hidden)),
        sds((width, rows), bf16),
    ]
    return kernel_call(
        expert_body,
        (steps,),
        (),
        (*xs, w_in, w_in, w_out),
        [whole(x.shape) for x in xs]
        + [
            pl.BlockSpec((width, blk), lambda i: (0, i)),
            pl.BlockSpec((width, blk), lambda i: (0, steps + i)),
            pl.BlockSpec((blk, width), lambda i: (i, 0)),
        ],
        outs,
        [whole((part, width))] * 4 + [col, col, col, whole((width, rows))],
        scratch=[pltpu.VMEM((rows, width), bf16), pltpu.VMEM((rows, width), f32)],
        flops=6 * rows * width * hidden,
        name="expert",
    )


def expert_back_body(z0, z1, z2, z3, wg, wu, wo, gates, ups, r0, r1, r2, r3, gg, ug, zout, zs, acc):
    step = pl.program_id(0)
    part = z0.shape[0]

    @pl.when(step == 0)
    def _():
        for j, z in enumerate((z0, z1, z2, z3)):
            zs[j * part : (j + 1) * part, :] = z[...]
        acc[...] = jnp.zeros(acc.shape, f32)
        zout[...] = zs[...]

    s = dot(zs[...], wo[...], 1, 1)
    act, dact = silu_parts(gates[...])
    gate_grad = (s * ups[...] * dact).astype(bf16)
    up_grad = (s * act).astype(bf16)
    gg[...] = gate_grad
    ug[...] = up_grad
    acc[...] += dot(gate_grad, wg[...], 1, 1) + dot(up_grad, wu[...], 1, 1)

    @pl.when(step == pl.num_programs(0) - 1)
    def _():
        for j, r in enumerate((r0, r1, r2, r3)):
            r[...] = acc[j * part : (j + 1) * part, :].astype(bf16)


def expert_back(zs, w_in, w_out, gates, ups):
    part, width = zs[0].shape
    rows = 4 * part
    hidden = w_out.shape[0]
    blk = 256
    steps = hidden // blk
    col = pl.BlockSpec((rows, blk), lambda i: (0, i))
    outs = [sds((part, width), bf16)] * 4 + [
        sds((rows, hidden), bf16),
        sds((rows, hidden), bf16),
        sds((rows, width), bf16),
    ]
    return kernel_call(
        expert_back_body,
        (steps,),
        (),
        (*zs, w_in, w_in, w_out, gates, ups),
        [whole(z.shape) for z in zs]
        + [
            pl.BlockSpec((width, blk), lambda i: (0, i)),
            pl.BlockSpec((width, blk), lambda i: (0, steps + i)),
            pl.BlockSpec((blk, width), lambda i: (i, 0)),
            col,
            col,
        ],
        outs,
        [whole((part, width))] * 4 + [col, col, whole((rows, width))],
        scratch=[pltpu.VMEM((rows, width), bf16), pltpu.VMEM((rows, width), f32)],
        flops=6 * rows * width * hidden,
        name="expert_back",
    )


def expert_in_grad_body(sc, xt, gg, ug, keep, send):
    step = pl.program_id(0)
    half = keep.shape[1]
    d = sc[8]
    pair = jnp.where(step < pl.num_programs(0) // 2, gg[...], ug[...])
    keep[0] = dot(xt[pl.ds(pl.multiple_of(d * half, 16), half), :], pair).astype(bf16)
    send[0] = dot(xt[pl.ds(pl.multiple_of((1 - d) * half, 16), half), :], pair).astype(bf16)


def expert_in_grad(sc, xt, gg, ug, groups):
    width, rows = xt.shape
    hidden = gg.shape[1]
    blk = 512
    steps = 2 * hidden // blk
    per = steps // groups
    last = steps // 2 - 1
    out = sds((groups, width // 2, 2 * hidden // groups), bf16)
    spec = pl.BlockSpec((1, width // 2, blk), lambda i, s: (i // per, 0, i % per))
    return kernel_call(
        expert_in_grad_body,
        (steps,),
        (sc,),
        (xt, gg, ug),
        [
            whole(xt.shape),
            pl.BlockSpec((rows, blk), lambda i, s: (0, jnp.minimum(i, last))),
            pl.BlockSpec((rows, blk), lambda i, s: (0, jnp.maximum(i - last - 1, 0))),
        ],
        [out, out],
        [spec, spec],
        flops=4 * width * rows * hidden,
        name="expert_in_grad",
    )


def expert_out_grad_body(sc, h, z, keep, send):
    g = dot(h[...].T, z[...]).astype(bf16)
    half = keep.shape[1]
    first = sc[8] == 0
    keep[...] = jnp.where(first, g[:, :half], g[:, half:])
    send[...] = jnp.where(first, g[:, half:], g[:, :half])


def expert_out_grad(sc, h, z):
    rows, hidden = h.shape
    width = z.shape[1]
    blk = 512
    out = sds((hidden, width // 2), bf16)
    spec = pl.BlockSpec((blk, width // 2), lambda i, s: (i, 0))
    return kernel_call(
        expert_out_grad_body,
        (hidden // blk,),
        (sc,),
        (h, z),
        [pl.BlockSpec((rows, blk), lambda i, s: (0, i)), whole(z.shape)],
        [out, out],
        [spec, spec],
        flops=2 * width * rows * hidden,
        name="expert_out_grad",
    )


def combine_body(r0, r1, r2, r3, selt, probs, residual, shared_res, cot, out, logit_grad):
    p = probs[...]
    acc = residual[...] + shared_res[...]
    c = cot[...].astype(f32)
    lane = lax.broadcasted_iota(jnp.int32, p.shape, 1)
    grad = jnp.zeros(p.shape, f32)
    for j, r in enumerate((r0, r1, r2, r3)):
        per = dot(selt[j], r[...])
        acc = acc + p[:, j : j + 1] * per
        grad = jnp.where(lane == j, jnp.sum(per * c, axis=-1, keepdims=True), grad)
    out[...] = acc.astype(bf16)
    logit_grad[...] = p * (grad - jnp.sum(p * grad, axis=-1, keepdims=True))


def combine(rs, selt, probs, residual, shared_res, cot):
    ins = (*rs, selt, probs, residual, shared_res, cot)
    outs = [sds(cot.shape, bf16), sds(probs.shape)]
    return kernel_call(
        combine_body,
        (1,),
        (),
        ins,
        [whole(i.shape) for i in ins],
        outs,
        [whole(i.shape) for i in outs],
        flops=8 * cot.size * selt.shape[2],
        name="combine",
    )


def feed_back_body(
    sc, r0, r1, r2, r3, selt, shared_back, logit_grad, router, residual, gain, cot, b,
    w0, w1, w2, w3, c0, c1, c2, c3,
    state, h0, h1, h2, h3, keep, send, small, wscr,
):
    part = w0.shape[0]
    for j, w in enumerate((w0, w1, w2, w3)):
        wscr[pl.ds(pl.multiple_of(sc[4 + j] * part, 16), part), :] = w[...]
    grad = shared_back[...]
    for j, r in enumerate((r0, r1, r2, r3)):
        grad = grad + dot(selt[j], r[...])
    lg = logit_grad[...]
    grad = grad + dot(lg, router[...].astype(f32), 1, 1, highest)
    rows4 = dot(lg, b[...].astype(f32), 0, 0, highest)
    v = residual[...]
    scale = lax.rsqrt(jnp.mean(v * v, axis=-1, keepdims=True) + epsilon)
    unit = v * scale
    small[...] = rows4[0:8, :]
    small[4:5, :] = jnp.sum(grad * unit, axis=0, keepdims=True)
    gg = grad * gain[...]
    total = cot[...].astype(f32) + scale * (gg - unit * jnp.mean(gg * unit, axis=-1, keepdims=True))
    state[...] = total
    branch = total.astype(bf16)
    head = c0.shape[1]
    e = sc[4]
    for j, (ctx, h) in enumerate(((c0, h0), (c1, h1), (c2, h2), (c3, h3))):
        at = pl.ds(pl.multiple_of(sc[j] * head, 16), head)
        h[...] = dot(branch, wscr[at, :], 1, 1).astype(bf16)
    for j, ctx in enumerate((c0, c1, c2, c3)):
        g = dot(ctx[...].T, branch).astype(bf16)
        place = jnp.bitwise_xor(e, sc[j])

        @pl.when(place % 2 == 0)
        def _(g=g, place=place):
            keep[place // 2] = g

        @pl.when(place % 2 == 1)
        def _(g=g, place=place):
            send[place // 2] = g


def feed_back(sc, rs, selt, shared_back, logit_grad, router, residual, gain, cot, b, ws, ctx):
    rows, width = cot.shape
    head = ctx[0].shape[1]
    ins = (*rs, selt, shared_back, logit_grad, router, residual, gain, cot, b, *ws, *ctx)
    outs = (
        [sds((rows, width))]
        + [sds((rows, head), bf16)] * 4
        + [sds((2, head, width), bf16)] * 2
        + [sds((8, width))]
    )
    return kernel_call(
        feed_back_body,
        (1,),
        (sc,),
        ins,
        [whole(i.shape) for i in ins],
        outs,
        [whole(i.shape) for i in outs],
        scratch=[pltpu.VMEM((width, width), bf16)],
        flops=2 * rows * width * width * 2 + 8 * rows * selt.shape[2] * width,
        name="feed_back",
    )


def tokens_grad_body(sc, m0, m1, m2, m3, w0, w1, w2, w3, x, gain, state, out, mscr, wscr):
    part = w0.shape[0]
    head = m0.shape[1] // 3
    width = x.shape[1]
    for j, w in enumerate((w0, w1, w2, w3)):
        wscr[pl.ds(pl.multiple_of(sc[4 + j] * part, 16), part), :] = w[...]
    ms = (m0, m1, m2, m3)
    for g in range(4):
        at = jnp.bitwise_xor(sc[0], g)
        piece = jnp.where(
            at == 0, ms[0][...], jnp.where(at == 1, ms[1][...], jnp.where(at == 2, ms[2][...], ms[3][...]))
        )
        for t in range(3):
            mscr[:, t * width + g * head : t * width + (g + 1) * head] = piece[:, t * head : (t + 1) * head]
    grad = dot(mscr[...], wscr[...], 1, 1)
    v = x[...].astype(f32)
    scale = lax.rsqrt(jnp.mean(v * v, axis=-1, keepdims=True) + epsilon)
    unit = v * scale
    gg = grad * gain[...]
    out[...] = state[...] + scale * (gg - unit * jnp.mean(gg * unit, axis=-1, keepdims=True))


def tokens_grad(sc, ms, ws, x, gain, state):
    rows, width = x.shape
    ins = (*ms, *ws, x, gain, state)
    outs = [sds((rows, width))]
    return kernel_call(
        tokens_grad_body,
        (1,),
        (sc,),
        ins,
        [whole(i.shape) for i in ins],
        outs,
        [whole(i.shape) for i in outs],
        scratch=[pltpu.VMEM((rows, 3 * width), bf16), pltpu.VMEM((width, 3 * width), bf16)],
        flops=6 * rows * width * width,
        name="tokens_grad",
    )[0]


def join_mixed_body(sc, p0, p1, p2, p3, w, gain, out, gain_grad):
    head = p0.shape[1] // 3
    width = out.shape[1] // 3
    ps = (p0, p1, p2, p3)
    for g in range(4):
        at = jnp.bitwise_xor(sc[0], g)
        piece = jnp.where(
            at == 0, ps[0][...], jnp.where(at == 1, ps[1][...], jnp.where(at == 2, ps[2][...], ps[3][...]))
        ).astype(f32)
        for t in range(3):
            out[:, t * width + g * head : t * width + (g + 1) * head] = piece[:, t * head : (t + 1) * head]
    total = jnp.sum(out[...] * w[...].astype(f32), axis=-1, keepdims=True)
    gain_grad[...] = jnp.broadcast_to(total / gain[...], gain_grad.shape)


def join_mixed(sc, ps, w, gain):
    ins = (*ps, w, gain)
    outs = [sds(w.shape), sds((w.shape[0], 128))]
    return kernel_call(
        join_mixed_body,
        (1,),
        (sc,),
        ins,
        [whole(i.shape) for i in ins],
        outs,
        [whole(i.shape) for i in outs],
        flops=2 * w.size,
        name="join_mixed",
    )


def join_rows_body(sc, p0, p1, p2, p3, out):
    part = p0.shape[0]
    for j, p in enumerate((p0, p1, p2, p3)):
        out[pl.ds(pl.multiple_of(sc[j] * part, 16), part), :] = p[...].astype(out.dtype)


def join_rows(sc, ps):
    part, width = ps[0].shape
    outs = [sds((4 * part, width))]
    return kernel_call(
        join_rows_body,
        (1,),
        (sc,),
        tuple(ps),
        [whole(p.shape) for p in ps],
        outs,
        [whole(o.shape) for o in outs],
        name="join_rows",
    )[0]


def join_halves_body(sc, *refs, side):
    pieces, out = refs[:-1], refs[-1]
    rows, width = out.shape
    part = pieces[0].shape[0]
    d = sc[8]
    mine, other = pieces[:4], pieces[4:]
    for j in range(4):
        for half, group in ((d, mine), (1 - d, other)):
            value = group[j][...].astype(f32)
            if side:
                at = pl.ds(pl.multiple_of(sc[j] * part, 16), part)

                @pl.when(half == 0)
                def _(value=value, at=at):
                    out[at, : width // 2] = value

                @pl.when(half == 1)
                def _(value=value, at=at):
                    out[at, width // 2 :] = value
            else:
                start = half * (rows // 2) + sc[j] * part
                out[pl.ds(pl.multiple_of(start, 16), part), :] = value


def join_halves(sc, mine, other, side):
    part, width = mine[0].shape
    shape = (4 * part, 2 * width) if side else (8 * part, width)
    ins = (*mine, *other)
    outs = [sds(shape)]
    return kernel_call(
        functools.partial(join_halves_body, side=side),
        (1,),
        (sc,),
        ins,
        [whole(i.shape) for i in ins],
        outs,
        [whole(o.shape) for o in outs],
        name="join_halves",
    )[0]


def pair_body(sc, mine, other, out, *, side):
    rows, width = out.shape
    first = sc[8] == 0
    a = mine[...].astype(f32)
    b = other[...].astype(f32)
    if side:
        out[:, : width // 2] = jnp.where(first, a, b)
        out[:, width // 2 :] = jnp.where(first, b, a)
    else:
        out[: rows // 2, :] = jnp.where(first, a, b)
        out[rows // 2 :, :] = jnp.where(first, b, a)


def pair(sc, mine, other, side):
    r, w = mine.shape
    shape = (r, 2 * w) if side else (2 * r, w)
    outs = [sds(shape)]
    return kernel_call(
        functools.partial(pair_body, side=side),
        (1,),
        (sc,),
        (mine, other),
        [whole(mine.shape), whole(other.shape)],
        outs,
        [whole(shape)],
        name="pair",
    )[0]


def gather_ep(x):
    two = swap(x, "ep", 2)
    return (x, swap(x, "ep", 1), two, swap(two, "ep", 1))


def add(*parts):
    total = parts[0].astype(f32)
    for p in parts[1:]:
        total = total + p.astype(f32)
    return total.astype(bf16)


def rest_of_dp(x):
    k = 2
    while k < lax.axis_size("dp"):
        x = add(x, swap(x, "dp", k))
        k *= 2
    return x


def scatter_rows(x, index):
    part = x.shape[0] // 4
    at = lambda k: lax.dynamic_slice_in_dim(x, (index ^ k) * part, part, 0)
    return add(at(0), *[swap(at(k), "ulysses", k) for k in (1, 2, 3)])


def gather_z(x):
    return (x, *[swap(x, "ulysses", k) for k in (1, 2, 3)])


def shards(
    tokens,
    lengths,
    permutation,
    routes,
    cotangent,
    attention_gain,
    attention_in,
    attention_out,
    feed_gain,
    router_weight,
    shared_in,
    shared_out,
    expert_in,
    expert_out,
):
    groups = lax.axis_size("ulysses")
    own_group = lax.axis_index("ulysses")
    own_ep = lax.axis_index("ep")
    own_dp = lax.axis_index("dp")
    low = own_dp & 1
    pack_number = own_dp * lax.axis_size("ep") + own_ep
    inputs = tokens[0]
    cot = cotangent[0]
    rows, width = inputs.shape
    pack_rows = rows * groups
    count_seqs = lengths.shape[1]
    experts = expert_in.shape[0] * lax.axis_size("ep")
    top = routes.shape[2]
    capacity = (9 * rows * top + 8 * experts - 1) // (8 * experts)
    slots = (capacity + 15) // 16 * 16
    heads = width // HEAD_DIM // groups
    wide = heads * HEAD_DIM
    four = jnp.arange(4, dtype=jnp.int32)
    sc = jnp.concatenate(
        [own_group ^ four, own_ep ^ four, jnp.stack([low, low, low, low])]
    ).astype(jnp.int32)

    xs = gather_z(inputs)
    small = jnp.concatenate(
        [attention_gain[None], feed_gain[None], router_weight.T, jnp.zeros((2, attention_gain.shape[0]), bf16)]
    )
    small_parts = gather_ep(small)
    mix_parts = gather_ep(attention_in)
    out_parts = gather_ep(attention_out)
    shared_in_parts = gather_ep(shared_in)
    shared_out_parts = gather_ep(shared_out)
    stacked = jnp.stack(small_parts)
    smalls = jnp.concatenate(
        [lax.dynamic_index_in_dim(stacked, own_ep ^ j, 0, False) for j in range(4)], axis=1
    )
    gain_one = smalls[0:1].astype(f32)
    gain_two = smalls[1:2].astype(f32)
    router = jnp.stack(
        [lax.dynamic_index_in_dim(smalls, 2 + (own_ep ^ j), 0, False) for j in range(4)], axis=1
    )
    router = jnp.pad(router, ((0, 0), (0, 124)))
    mine_of = lambda w: lax.dynamic_index_in_dim(
        w.reshape(-1, 3, groups, wide), own_group, 2, False
    ).reshape(-1, 3 * wide)
    head_parts = [mine_of(w) for w in mix_parts]

    ends = jnp.cumsum(lengths[0])
    begins = ends - lengths[0]
    index = jnp.arange(pack_rows, dtype=jnp.int32)
    segment = jnp.sum((index[:, None] >= ends[None, :]).astype(jnp.int32), axis=1, dtype=jnp.int32)
    which = segment[:, None] == jnp.arange(count_seqs, dtype=jnp.int32)[None, :]
    begin = jnp.sum(jnp.where(which, begins[None, :], 0), axis=1, dtype=jnp.int32)
    end = jnp.sum(jnp.where(which, ends[None, :], 0), axis=1, dtype=jnp.int32)
    starts = jnp.broadcast_to(begin[None, :], (8, pack_rows))
    lo = begin[0::QB] // KB
    hi = (end[KB - 1 :: KB] + QB - 1) // QB
    half = HEAD_DIM // 2
    freq = base_freq ** (-(jnp.arange(half, dtype=f32) * 2.0) / HEAD_DIM)
    angle = (index - begin).astype(f32)[:, None] * jnp.tile(freq, 4)[None, :]
    sign = jnp.tile(jnp.repeat(jnp.array([-1.0, 1.0], f32), half), 2)
    cos = jnp.cos(angle)
    sin = jnp.sin(angle) * sign[None, :]

    seq_rank = lax.dynamic_slice_in_dim(permutation, pack_number * count_seqs, count_seqs)
    own_rows = own_group * rows + jnp.arange(rows, dtype=jnp.int32)
    own_which = lax.dynamic_slice_in_dim(which, own_group * rows, rows, 0)
    priority = (
        jnp.sum(jnp.where(own_which, seq_rank[None, :], 0), axis=1, dtype=jnp.int32) * pack_rows
        + own_rows
    )
    member = jnp.sum(
        (routes[0][:, :, None] == (own_ep ^ jnp.arange(experts, dtype=jnp.int32))[None, None, :]).astype(f32),
        axis=1,
    )
    earlier = (priority[None, :] < priority[:, None]).astype(bf16)
    rank = jnp.dot(earlier, member.astype(bf16), preferred_element_type=f32)
    keep = member * (rank < capacity).astype(f32)
    numbers = jnp.arange(slots, dtype=f32)
    selt = (
        keep.T[:, :, None] * (rank.T[:, :, None] == numbers[None, None, :]).astype(f32)
    ).astype(bf16)
    sel = (
        keep.T[:, None, :] * (rank.T[:, None, :] == numbers[None, :, None]).astype(f32)
    ).astype(bf16)

    q, k, kt, v, vt, at = qkv(sc, xs, head_parts, gain_one, cos, sin, heads)
    *att, o, lse = attend(sc, lo, q, k, vt, starts, rows)
    ctx = [att[0]] + [swap(att[j], "ulysses", j) for j in (1, 2, 3)]

    residual, b, bt, probs, *sent = feed(
        sc, ctx, out_parts, inputs, gain_two, router, sel, cot
    )
    across = lambda ps: [ps[0]] + [swap(ps[j], "ep", j) for j in (1, 2, 3)]
    received = across(sent[:4])
    slot_grads = across(sent[4:])
    shared_res, shared_back, in_keep, in_send, so_grad = shared(
        sc, b, bt, cot, shared_in_parts, shared_out_parts
    )
    w_in, w_out = expert_in[0], expert_out[0]
    *results, hidden, gates, ups, xt = expert(received, w_in, w_out)
    returned = across(results)
    *row_grads, gg, ug, zs = expert_back(slot_grads, w_in, w_out, gates, ups)
    row_back = across(row_grads)
    ei_keep, ei_send = expert_in_grad(sc, xt, gg, ug, groups)
    eo_keep, eo_send = expert_out_grad(sc, hidden, zs)

    output, logit_grad = combine(returned, selt, probs, residual, shared_res, cot)
    state, a0, a1, a2, a3, ao_keep, ao_send, tiny = feed_back(
        sc, row_back, selt, shared_back, logit_grad, router, residual, gain_two, cot, b,
        out_parts, ctx,
    )
    head_grads = [a0] + [swap(a, "ulysses", j) for j, a in ((1, a1), (2, a2), (3, a3))]
    *mixed_parts, mixed = attend_back(
        sc, hi, q, k, kt, v, lse, o, starts, head_grads, cos, sin
    )
    mixed_rows = [mixed_parts[0]] + [swap(mixed_parts[j], "ulysses", j) for j in (1, 2, 3)]
    mi_keep, mi_send = mixed_weight_grad(sc, at, mixed)
    grad_tokens = tokens_grad(sc, mixed_rows, mix_parts, inputs, gain_one, state)

    s = add(in_keep, swap(in_send, "ep", 1))
    part = s.shape[1] // 2
    s = add(s[:, :part], swap(s[:, part:], "ep", 2))
    pick = lambda x, i: lax.dynamic_index_in_dim(x, i, 0, False)
    s = rest_of_dp(add(pick(s, low), swap(pick(s, 1 - low), "dp", 1)))
    mine = gather_z(scatter_rows(s, own_group))
    other = [swap(p, "dp", 1) for p in mine]
    share_shared_in = join_halves(sc, mine, other, True)

    s = so_grad.reshape(4, -1, width)
    s_keep = add(s[0], swap(s[1], "ep", 1))
    s_send = add(s[2], swap(s[3], "ep", 1))
    s = add(s_keep, swap(s_send, "ep", 2)).reshape(2, -1, width)
    s = rest_of_dp(add(pick(s, low), swap(pick(s, 1 - low), "dp", 1)))
    mine = gather_z(scatter_rows(s, own_group))
    other = [swap(p, "dp", 1) for p in mine]
    share_shared_out = join_halves(sc, mine, other, False)

    s = rest_of_dp(add(ei_keep, swap(ei_send, "dp", 1)))
    s = add(pick(s, own_group), *[swap(pick(s, own_group ^ j), "ulysses", j) for j in (1, 2, 3)])
    expert_in_grads = pair(sc, s, swap(s, "dp", 1), False)[None]
    s = rest_of_dp(add(eo_keep, swap(eo_send, "dp", 1)))
    s = scatter_rows(s, own_group)
    expert_out_grads = pair(sc, s, swap(s, "dp", 1), True)[None]

    def ep_then_all(keep, send):
        s = add(keep, swap(send, "ep", 1))
        s = add(s[0], swap(s[1], "ep", 2))
        return rest_of_dp(add(s, swap(s, "dp", 1)))

    s = ep_then_all(ao_keep, ao_send)
    share_out = join_rows(sc, gather_z(scatter_rows(s, own_group)))

    s = ep_then_all(mi_keep, mi_send)
    share_in, share_gain = join_mixed(
        sc, gather_z(s), attention_in, attention_gain.astype(f32)[:, None]
    )
    share_gain_first = share_gain[:, 0]

    t = jnp.concatenate([jnp.take(tiny[0:4], own_ep ^ four, axis=0), tiny[4:8]])
    for axis in ("ep", "ulysses", "dp"):
        k = 1
        while k < lax.axis_size(axis):
            t = t + swap(t, axis, k)
            k *= 2
    t = lax.dynamic_slice_in_dim(t, own_ep * (width // 4), width // 4, 1)
    share_router = t[0:experts].T
    share_gain_second = t[4]

    return (
        output[None],
        grad_tokens[None],
        share_gain_first,
        share_in,
        share_out,
        share_gain_second,
        share_router,
        share_shared_in,
        share_shared_out,
        expert_in_grads,
        expert_out_grads,
    )


def solution(mesh):
    placed = (
        P(("dp", "ep"), "ulysses", None),
        P(("dp", "ep"), None),
        P(),
        P(("dp", "ep"), "ulysses", None),
        P(("dp", "ep"), "ulysses", None),
        P("ep"),
        P("ep", None),
        P("ep", None),
        P("ep"),
        P("ep", None),
        P("ep", None),
        P("ep", None),
        P("ep", None, None),
        P("ep", None, None),
    )
    return jax.shard_map(
        shards,
        mesh=mesh,
        in_specs=placed,
        out_specs=(
            P(("dp", "ep"), "ulysses", None),
            P(("dp", "ep"), "ulysses", None),
            P("ep"),
            P("ep", None),
            P("ep", None),
            P("ep"),
            P("ep", None),
            P("ep", None),
            P("ep", None),
            P("ep", None, "ulysses"),
            P("ep", "ulysses", None),
        ),
        check_vma=False,
    )
```
